256 devices in a mesh: pair: 32 (over z_hi, x, core), row: 8 (over y, z_lo).
Axes of the slice: x: 4, y: 4, z: 8 (z_hi: 4, z_lo: 2; z = z_hi * 2 + z_lo), core: 2. Of those that a mesh axis runs over, the one named last changes fastest.
Arguments:
- gram_field: float32 [128, 8, 16, 16, 256], P('pair', None, 'row'), may hold values from -3.6 to 3.6, as said below
- left_variance: float32 [128, 16, 16], P('pair'), may hold values from 0.25 to 4
- right_variance: float32 [8, 16, 16], replicated, may hold values from 0.25 to 4
- cotangent: float32 [128, 8, 8, 8, 64], P('pair', 'row'), may hold values from -24 to 24
Outputs:
- gram_gradient: float32 [128, 8, 16, 16, 256], P('pair', None, 'row')
- left_gradient: float32 [128, 16, 16], P('pair')
- right_gradient: float32 [8, 16, 16], replicated
The draws below stay inside these ranges and needn't reach their ends.
Inputs may be any that keep to these rules, and one draw needn't show every extreme that they name: `gram_field`: each entry lies within 0.9 times the square root of the product of left_variance and right_variance at its two pixels.
All inputs are finite; a program needn't handle non-finite values.
Results may differ from the reference program's by a relative error of at most 0.00008.
Values sent between devices are 32-bit elements; how exact they have to be, the bound alone decides.
No kernel may reach another device: no remote copies, remote signals or barrier semaphores. Data moves between devices by JAX's collectives and lax.ppermute only.
A program may use at most 64 MiB of HBM per device.

```python
import math
import jax
import jax.numpy as jnp
from jax import lax

R = 16
H = 8
A = 128
B = 8


def shared_variances(key):
    key_left = jax.random.fold_in(key, 11)
    key_right = jax.random.fold_in(key, 12)
    low = math.log(0.25)
    high = math.log(4.0)
    left = jnp.exp(jax.random.uniform(key_left, (A, R, R), jnp.float32, low, high))
    right = jnp.exp(jax.random.uniform(key_right, (B, R, R), jnp.float32, low, high))
    return (left, right)


def draw_left_variance(key, part):
    return shared_variances(key)[0]


def draw_right_variance(key, part):
    return shared_variances(key)[1]


def draw_gram_field(key, part):
    left, right = shared_variances(key)
    key_ratio = jax.random.fold_in(key, 13)
    ratio = jax.random.uniform(key_ratio, (A, B, R, R, R * R), jnp.float32, -0.9, 0.9)
    left_root = jnp.sqrt(left)[:, None, :, :, None]
    right_root = jnp.sqrt(right).reshape(1, B, 1, 1, R * R)
    return left_root * right_root * ratio


def shard_levels(key, shape, cuts, smallest, largest):
    def one(dim, shards_of):
        draws = jax.random.uniform(jax.random.fold_in(jax.random.fold_in(key, 6), dim), (shards_of,), jnp.float32, smallest / len(cuts), largest / len(cuts))
        return jnp.repeat(jnp.exp(draws), shape[dim] // shards_of).reshape((-1,) + (1,) * (len(shape) - dim - 1))

    factor_of = one(*cuts[0])
    for cut in cuts[1:]:
        factor_of = factor_of * one(*cut)
    return factor_of


def scatter_about(key, dims, width, bound, split=(), held_as=jnp.bfloat16):
    array = width * jax.random.normal(key, dims, jnp.float32)
    if split:
        array = array * shard_levels(key, dims, split, -0.22, 0.18)
    return jnp.clip(array, -bound, bound).astype(held_as)


def setup_inputs(seed: int = 0) -> dict:
    seeds = jax.random.split(jax.random.key(seed), 5)
    gram_field = draw_gram_field(jax.random.fold_in(seeds[4], 71), 0)
    left_variance = draw_left_variance(jax.random.fold_in(seeds[4], 71), 0)
    right_variance = draw_right_variance(jax.random.fold_in(seeds[4], 71), 0)
    cotangent = scatter_about(seeds[3], (A, B, H, H, H * H), 4.0, 24.0, ((0, 32), (1, 8)), jnp.float32)
    return dict(gram_field=gram_field, left_variance=left_variance, right_variance=right_variance, cotangent=cotangent)


def shifted(source, dimension, offset):
    dimension = dimension % source.ndim
    extent = source.shape[dimension]
    margin = abs(offset)
    widths = [(0, 0)] * source.ndim
    widths[dimension] = (margin, margin)
    padded = jnp.pad(source, widths)
    return lax.slice_in_dim(padded, margin + offset, margin + offset + extent, axis=dimension)

def column_masks(length):
    column_index = jnp.arange(length * length) % length
    return ((column_index + 1 < length).astype(jnp.float32), (column_index >= 1).astype(jnp.float32))

def mix_columns(source, length):
    mask_up, mask_down = column_masks(length)
    return source + shifted(shifted(source, -2, 1), -1, 1) * mask_up + shifted(shifted(source, -2, -1), -1, -1) * mask_down

def conv_field(padded, length):
    inner = padded[..., 1:-1, :, :] + shifted(padded[..., 2:, :, :], -1, length) + shifted(padded[..., :-2, :, :], -1, -length)
    return mix_columns(inner, length) / 9.0

def pad_rows(source):
    widths = [(0, 0)] * source.ndim
    widths[source.ndim - 3] = (1, 1)
    return jnp.pad(source, widths)

def conv_map(source):
    row_sum = source + shifted(source, -2, 1) + shifted(source, -2, -1)
    return (row_sum + shifted(row_sum, -1, 1) + shifted(row_sum, -1, -1)) / 9.0

def pool_field(source):
    shape = source.shape
    leading = shape[:-3]
    count = shape[-3]
    length = shape[-2]
    half_side = length // 2
    merged = source.reshape(shape[:-1] + (half_side, 2 * length))
    merged = merged[..., :length] + merged[..., length:]
    merged = merged.reshape(shape[:-1] + (half_side * length,))
    merged = merged[..., 0::2] + merged[..., 1::2]
    merged = merged.reshape(leading + (count // 2, 2, half_side, 2, half_side * half_side))
    return lax.optimization_barrier(jnp.sum(merged, axis=(-4, -2))) / 16.0

def spread_field(source):
    half_side = source.shape[-2]
    merged = jnp.repeat(source, 2, axis=-3)
    merged = jnp.repeat(merged, 2, axis=-2)
    inner = merged.shape[:-1]
    merged = merged.reshape(inner + (half_side, 1, half_side, 1))
    merged = jnp.broadcast_to(merged, inner + (half_side, 2, half_side, 2))
    return merged.reshape(inner + (4 * half_side * half_side,)) / 16.0

def pool_map(source):
    extent = source.shape[-1] // 2
    merged = source.reshape(source.shape[:-2] + (extent, 2, extent, 2))
    return lax.optimization_barrier(jnp.mean(merged, axis=(-3, -1)))

def spread_map(source):
    return jnp.repeat(jnp.repeat(source, 2, axis=-2), 2, axis=-1) / 4.0

def arc_kernel(source, left, right):
    magnitude = jnp.sqrt(left * right)
    cosine = source / magnitude
    angle_part = jnp.pi - jnp.arccos(cosine)
    sine_part = jnp.sqrt(1.0 - cosine * cosine)
    kernel = magnitude * (sine_part + angle_part * cosine) / (2.0 * jnp.pi)
    slopes = angle_part / (2.0 * jnp.pi)
    weights = magnitude * sine_part / (4.0 * jnp.pi)
    return (kernel, slopes, weights)

def reference(gram_field, left_variance, right_variance, cotangent):
    length = gram_field.shape[3]
    half_side = length // 2
    count = right_variance.shape[0]
    first_right = conv_map(right_variance)
    right_flat = first_right.reshape(count, 1, 1, length * length)
    second_right = conv_map(pool_map(first_right / 2.0))
    second_flat = second_right.reshape(count, 1, 1, half_side * half_side)

    def one_image(items):
        gram_one, variance_one, cot_one = items
        first_left = conv_map(variance_one)
        source_one = conv_field(pad_rows(gram_one), length)
        kernel_one, slope_one, weight_one = arc_kernel(source_one, first_left[None, :, :, None], right_flat)
        second_left = conv_map(pool_map(first_left / 2.0))
        source_two = conv_field(pad_rows(pool_field(kernel_one)), half_side)
        unused, slope_two, weight_two = arc_kernel(source_two, second_left[None, :, :, None], second_flat)
        weighted_two = cot_one * weight_two
        left_two = lax.optimization_barrier(jnp.sum(weighted_two, axis=(0, 3))) / second_left
        right_two = lax.optimization_barrier(jnp.sum(weighted_two, axis=(1, 2))) / second_flat.reshape(count, half_side * half_side)
        back_one = spread_field(conv_field(pad_rows(cot_one * slope_two), half_side))
        weighted_one = back_one * weight_one
        left_one = spread_map(conv_map(left_two)) / 2.0 + lax.optimization_barrier(jnp.sum(weighted_one, axis=(0, 3))) / first_left
        right_local = lax.optimization_barrier(jnp.sum(weighted_one, axis=(1, 2))) / right_flat.reshape(count, length * length)
        right_one = spread_map(conv_map(right_two.reshape(count, half_side, half_side))) / 2.0 + right_local.reshape(count, length, length)
        gram_grad = conv_field(pad_rows(back_one * slope_one), length)
        return (gram_grad, conv_map(left_one), right_one)
    gram_gradient, left_gradient, right_parts = lax.map(one_image, (gram_field, left_variance, cotangent))
    right_gradient = conv_map(lax.optimization_barrier(jnp.sum(right_parts, axis=0)))
    return (gram_gradient, left_gradient, right_gradient)
```

```python
import functools
import math

import jax
import jax.numpy as jnp
from jax import lax
from jax.experimental import pallas as pl
from jax.experimental.pallas import tpu as pltpu
from jax.sharding import PartitionSpec as P


ARC = (
    1.570796251296997,
    -0.21459950506687164,
    0.08899294584989548,
    -0.05027513951063156,
    0.03123188205063343,
    -0.017667949199676514,
    0.00715474970638752,
    -0.0014201662270352244,
)
F32 = jnp.float32
BF16 = jnp.bfloat16


def shifted(source, dimension, offset):
    dimension = dimension % source.ndim
    extent = source.shape[dimension]
    margin = abs(offset)
    widths = [(0, 0)] * source.ndim
    widths[dimension] = (margin, margin)
    padded = jnp.pad(source, widths)
    return lax.slice_in_dim(padded, margin + offset, margin + offset + extent, axis=dimension)


def conv_map(source):
    row_sum = source + shifted(source, -2, 1) + shifted(source, -2, -1)
    return (row_sum + shifted(row_sum, -1, 1) + shifted(row_sum, -1, -1)) / 9.0


def pool_map(source):
    extent = source.shape[-1] // 2
    merged = source.reshape(source.shape[:-2] + (extent, 2, extent, 2))
    return jnp.mean(merged, axis=(-3, -1))


def spread_map(source):
    return jnp.repeat(jnp.repeat(source, 2, axis=-2), 2, axis=-1) / 4.0


def angle_and_sine(cosine):
    size = jnp.abs(cosine)
    rest = 1.0 - size
    square = rest * (1.0 + size)
    sine = square * lax.rsqrt(square)
    poly = jnp.full_like(size, ARC[-1])
    for factor in ARC[-2::-1]:
        poly = poly * size + factor
    arc = rest * lax.rsqrt(rest) * poly
    return jnp.where(cosine >= 0.0, math.pi - arc, arc), sine


def split_dot(value, matrix):
    high = value.astype(BF16)
    rest = value - high.astype(F32)
    middle = rest.astype(BF16)
    low = (rest - middle.astype(F32)).astype(BF16)
    dot = functools.partial(jnp.dot, preferred_element_type=F32)
    return dot(high, matrix) + dot(middle, matrix) + dot(low, matrix)


def fine_masks():
    lane = lax.broadcasted_iota(jnp.int32, (16, 128), 1)
    row = lax.broadcasted_iota(jnp.int32, (16, 128), 0)
    return (
        lane < 112,
        lane >= 16,
        (lane % 16 < 15) & (row < 15),
        (lane % 16 >= 1) & (row >= 1),
    )


def above(pair, masks):
    low, high = (pltpu.roll(v, 112, 1) for v in pair)
    return jnp.where(masks[0], low, high), jnp.where(masks[0], high, 0.0)


def below(pair, masks):
    low, high = (pltpu.roll(v, 16, 1) for v in pair)
    return jnp.where(masks[1], low, 0.0), jnp.where(masks[1], high, low)


def mixed(v, masks):
    up = pltpu.roll(pltpu.roll(v, 127, 1), 15, 0)
    down = pltpu.roll(pltpu.roll(v, 1, 1), 1, 0)
    return v + jnp.where(masks[2], up, 0.0) + jnp.where(masks[3], down, 0.0)


def fine_conv(rows, masks):
    before, now = None, rows(0)
    for i in range(16):
        after = rows(i + 1) if i < 15 else None
        total = now
        if after is not None:
            total = tuple(a + b for a, b in zip(total, above(after, masks)))
        if before is not None:
            total = tuple(a + b for a, b in zip(total, before))
        yield i, tuple(mixed(v, masks) for v in total)
        before, now = below(now, masks), after


def coarse_conv(rows, masks):
    out = []
    for i in range(8):
        total = rows[i]
        if i < 7:
            total = total + jnp.where(masks[0], pltpu.roll(rows[i + 1], 120, 1), 0.0)
        if i > 0:
            total = total + jnp.where(masks[1], pltpu.roll(rows[i - 1], 8, 1), 0.0)
        up = pltpu.roll(pltpu.roll(total, 127, 1), 14, 0)
        down = pltpu.roll(pltpu.roll(total, 1, 1), 2, 0)
        out.append(total + jnp.where(masks[2], up, 0.0) + jnp.where(masks[3], down, 0.0))
    return out


def body(
    field,
    left_root,
    left_inverse,
    right_maps,
    coarse_maps,
    second_scale,
    pools,
    spreads,
    lift,
    product,
    left_sums,
    right_sums,
    angles,
    sines,
    work,
    pooled,
    back,
):
    masks = fine_masks()
    halves = (slice(0, 128), slice(128, 256))
    inverse = [jnp.broadcast_to(right_maps[0:1, h], (16, 128)) for h in halves]
    scaled = [jnp.broadcast_to(right_maps[1:2, h], (16, 128)) for h in halves]
    root = [jnp.broadcast_to(right_maps[2:3, h], (16, 128)) for h in halves]

    def forward(a, carry):
        def rows(i):
            return tuple(field[i // 2, a, i % 2, :, h] for h in halves)

        held = None
        for i, source in fine_conv(rows, masks):
            scale = left_inverse[a, i]
            factor = left_root[a, i]
            kernel = []
            for n, h in enumerate(halves):
                cosine = source[n] * (scale * inverse[n])
                angle, sine = angle_and_sine(cosine)
                angles[a, i, :, h] = angle
                sines[a, i, :, h] = sine
                kernel.append((sine + angle * cosine) * (factor * scaled[n]))
            if i % 2:
                for n, h in enumerate(halves):
                    work[(i // 2) * 16 : (i // 2) * 16 + 16, h] = held[n] + kernel[n]
            held = kernel
        pooled[a] = split_dot(work[...], pools[a % 2])
        return carry

    lax.fori_loop(0, 4, forward, 0)

    lane = lax.broadcasted_iota(jnp.int32, (16, 128), 1)
    row = lax.broadcasted_iota(jnp.int32, (16, 128), 0)
    even = row % 2 == 0
    coarse_masks = (
        lane % 64 < 56,
        lane % 64 >= 8,
        (lane % 8 < 7) & (row < 14),
        (lane % 8 >= 1) & (row >= 2),
    )
    spot = lax.broadcasted_iota(jnp.int32, (8, 128), 1)
    second_left = jnp.zeros((8, 128), F32)
    second_right = jnp.zeros((16, 128), F32)
    for p in range(2):
        joined = pooled[2 * p] + pooled[2 * p + 1]
        level = []
        for i in range(8):
            v = joined[i * 16 : i * 16 + 16]
            level.append(v + jnp.where(even, pltpu.roll(v, 15, 0), pltpu.roll(v, 1, 0)))
        source = coarse_conv(level, coarse_masks)
        level = []
        for i in range(8):
            angle, sine = angle_and_sine(source[i] * coarse_maps[0, p, i])
            weighted = coarse_maps[1, p, i] * sine
            second_right = second_right + weighted
            for side in range(2):
                kept = jnp.where((lane < 64) == (side == 0), weighted, 0.0)
                total = jnp.sum(kept, axis=1, keepdims=True)
                for j in range(2):
                    place = ((2 * p + side) * 8 + i) * 2 + j
                    second_left = jnp.where(spot == place, total[j * 8 : j * 8 + 8], second_left)
            level.append(coarse_maps[2, p, i] * angle)
        for i, v in enumerate(coarse_conv(level, coarse_masks)):
            back[p, i * 16 : i * 16 + 16] = v

    def backward(a, carry):
        left_total, right_low, right_high = carry
        work[...] = split_dot(back[a // 2], spreads[a % 2])
        right = [right_low, right_high]
        for i in range(16):
            factor = left_root[a, i]
            across = None
            for n, h in enumerate(halves):
                coarse = work[(i // 2) * 16 : (i // 2) * 16 + 16, h]
                product[a, i, :, h] = coarse * angles[a, i, :, h] * (1.0 / (18.0 * math.pi))
                weighted = coarse * sines[a, i, :, h]
                right[n] = right[n] + weighted * factor
                term = weighted * root[n]
                across = term if across is None else across + term
            total = jnp.sum(across, axis=1, keepdims=True)
            for j in range(2):
                place = a * 32 + i * 2 + j
                left_total = jnp.where(spot == place, total[j * 8 : j * 8 + 8], left_total)
        return left_total, right[0], right[1]

    zero = jnp.zeros((16, 128), F32)
    left_total, *right = lax.fori_loop(
        0, 4, backward, (jnp.zeros((8, 128), F32), zero, zero)
    )
    left_sums[:, 0:128] = left_total
    left_sums[:, 128:256] = second_left
    two = jnp.sum(second_right, axis=0, keepdims=True) * second_scale[...]
    lifted = jnp.dot(
        two, lift[...], precision=lax.Precision.HIGHEST, preferred_element_type=F32
    )
    for n, h in enumerate(halves):
        one = jnp.sum(right[n], axis=0, keepdims=True) * right_maps[3:4, h]
        right_sums[:, h] = jnp.broadcast_to(one + lifted[0:1, h], (256, 128))


def last_conv(product, left_sums, blocks):
    masks = fine_masks()
    halves = (slice(0, 128), slice(128, 256))

    def image(a, carry):
        def rows(i):
            return tuple(product[a, i, :, h] for h in halves)

        for i, source in fine_conv(rows, masks):
            first = pl.multiple_of(a * 32 + (i % 2) * 16, 16)
            for n, h in enumerate(halves):
                blocks[i // 2, pl.ds(first, 16), h] = source[n]
        return carry

    lax.fori_loop(0, 4, image, 0)
    for target in range(8):
        blocks[target, 128:136, :] = left_sums[...]


def finish_right(sums, matrix, out):
    total = jnp.zeros((8, 256), F32)
    for p in range(32):
        total = total + sums[p * 8 : p * 8 + 8, :]
    mapped = jnp.dot(
        total, matrix[...], precision=lax.Precision.HIGHEST, preferred_element_type=F32
    )
    for k in range(16):
        out[:, k, :] = mapped[:, k * 16 : k * 16 + 16]


VMEM = pl.BlockSpec(memory_space=pltpu.VMEM)


def call(kernel, out_shapes, scratch=(), inputs=1):
    shapes = tuple(jax.ShapeDtypeStruct(s, F32) for s in out_shapes)
    return pl.pallas_call(
        kernel,
        out_shape=shapes if len(shapes) > 1 else shapes[0],
        in_specs=[VMEM] * inputs,
        out_specs=(VMEM,) * len(shapes) if len(shapes) > 1 else VMEM,
        scratch_shapes=[pltpu.VMEM(s, F32) for s in scratch],
    )


def near(rows, columns):
    close = (jnp.abs(rows[0][:, None] - columns[0][None, :]) <= 1) & (
        jnp.abs(rows[1][:, None] - columns[1][None, :]) <= 1
    )
    return close.astype(F32) / 9.0


def on_device(gram_field, left_variance, right_variance, cotangent):
    rank = lax.axis_index("row")
    sent = jnp.transpose(gram_field, (1, 0, 2, 3, 4))
    field = lax.all_to_all(sent, "row", split_axis=0, concat_axis=0, tiled=True)

    first_left = conv_map(left_variance)
    own_right = lax.dynamic_slice_in_dim(right_variance, rank, 1, axis=0)
    first_right = conv_map(own_right)
    second_left = conv_map(pool_map(first_left / 2.0))
    second_right = conv_map(pool_map(first_right / 2.0)).reshape(64)
    left_root = jnp.broadcast_to(jnp.sqrt(first_left)[..., None], (4, 16, 16, 128))
    left_inverse = jnp.broadcast_to(
        (1.0 / (9.0 * jnp.sqrt(first_left)))[..., None], (4, 16, 16, 128)
    )
    right_root = jnp.sqrt(first_right).reshape(1, 256)
    right_maps = jnp.concatenate(
        [
            1.0 / right_root,
            right_root / (32.0 * math.pi),
            right_root,
            1.0 / (4.0 * math.pi * right_root),
        ]
        * 2,
        axis=0,
    )

    def packed(v):
        v = jnp.repeat(v.reshape(2, 2, 8, 8, 64), 2, axis=3)
        return jnp.concatenate([v[:, 0], v[:, 1]], axis=-1)

    second = jnp.sqrt(second_left)[..., None] * jnp.sqrt(second_right)
    cotangent = cotangent[:, 0]
    coarse_maps = jnp.stack(
        [
            packed(1.0 / (9.0 * second)),
            packed(cotangent * second / (4.0 * math.pi)),
            packed(cotangent / (2.0 * math.pi * 9.0 * 16.0)),
        ]
    )
    second_scale = jnp.broadcast_to(jnp.tile(0.5 / second_right, 2)[None], (1, 128))

    fine = jnp.arange(256)
    small = jnp.arange(64)
    coarse_of = (fine // 32) * 8 + (fine % 16) // 2
    pool = (coarse_of[:, None] == small[None, :]).astype(BF16)
    nothing = jnp.zeros_like(pool)
    pools = jnp.stack(
        [jnp.concatenate([pool, nothing], 1), jnp.concatenate([nothing, pool], 1)]
    )
    spreads = jnp.transpose(pools, (0, 2, 1))
    lift = near((small // 8, small % 8), (coarse_of // 8, coarse_of % 8)) / 8.0
    lift = jnp.concatenate([lift, lift], axis=0)
    around = near((fine // 16, fine % 16), (fine // 16, fine % 16))

    product, left_sums, right_sums = call(
        body,
        ((4, 16, 16, 256), (8, 256), (256, 256)),
        (
            (4, 16, 16, 256),
            (4, 16, 16, 256),
            (128, 256),
            (4, 128, 128),
            (2, 128, 128),
        ),
        9,
    )(
        field,
        left_root,
        left_inverse,
        right_maps,
        coarse_maps,
        second_scale,
        pools,
        spreads,
        lift,
    )
    right_all = lax.all_to_all(
        right_sums, ("pair", "row"), split_axis=0, concat_axis=0, tiled=True
    )
    blocks = call(last_conv, ((8, 136, 256),), (), 2)(product, left_sums)
    blocks = lax.all_to_all(blocks, "row", split_axis=0, concat_axis=0, tiled=True)
    gram_gradient = jnp.transpose(blocks[:, :128].reshape(8, 4, 2, 16, 256), (1, 0, 2, 3, 4))

    left_all = jnp.sum(blocks[:, 128:], axis=0)
    left_one = left_all[:, :128].reshape(8, 4, 16, 2).transpose(1, 2, 3, 0).reshape(4, 16, 16)
    left_two = left_all[:, 128:192].reshape(4, 2, 4, 8, 2)[:, 0]
    left_two = left_two.transpose(1, 2, 3, 0).reshape(4, 8, 8)
    left_one = left_one / (4.0 * math.pi * jnp.sqrt(first_left))
    left_one = left_one + spread_map(conv_map(left_two / second_left)) / 2.0
    right_gradient = call(finish_right, ((8, 16, 16),), (), 2)(right_all, around)
    return gram_gradient, conv_map(left_one), right_gradient


def solution(mesh):
    in_specs = (
        P("pair", None, "row", None, None),
        P("pair", None, None),
        P(),
        P("pair", "row", None, None, None),
    )
    out_specs = (P("pair", None, "row", None, None), P("pair", None, None), P())
    return jax.shard_map(
        on_device, mesh=mesh, in_specs=in_specs, out_specs=out_specs, check_vma=False
    )
```

```python
import functools
import math

import jax
import jax.numpy as jnp
from jax import lax
from jax.experimental import pallas as pl
from jax.experimental.pallas import tpu as pltpu
from jax.sharding import PartitionSpec as P


ARC = (
    1.570796251296997,
    -0.21459950506687164,
    0.08899294584989548,
    -0.05027513951063156,
    0.03123188205063343,
    -0.017667949199676514,
    0.00715474970638752,
    -0.0014201662270352244,
)
F32 = jnp.float32
BF16 = jnp.bfloat16


def shifted(source, dimension, offset):
    dimension = dimension % source.ndim
    extent = source.shape[dimension]
    margin = abs(offset)
    widths = [(0, 0)] * source.ndim
    widths[dimension] = (margin, margin)
    padded = jnp.pad(source, widths)
    return lax.slice_in_dim(padded, margin + offset, margin + offset + extent, axis=dimension)


def conv_map(source):
    row_sum = source + shifted(source, -2, 1) + shifted(source, -2, -1)
    return (row_sum + shifted(row_sum, -1, 1) + shifted(row_sum, -1, -1)) / 9.0


def pool_map(source):
    extent = source.shape[-1] // 2
    merged = source.reshape(source.shape[:-2] + (extent, 2, extent, 2))
    return jnp.mean(merged, axis=(-3, -1))


def spread_map(source):
    return jnp.repeat(jnp.repeat(source, 2, axis=-2), 2, axis=-1) / 4.0


def angle_and_sine(cosine):
    size = jnp.abs(cosine)
    rest = 1.0 - size
    square = rest * (1.0 + size)
    sine = square * lax.rsqrt(square)
    poly = jnp.full_like(size, ARC[-1])
    for factor in ARC[-2::-1]:
        poly = poly * size + factor
    arc = rest * lax.rsqrt(rest) * poly
    return jnp.where(cosine >= 0.0, math.pi - arc, arc), sine


def split_dot(value, matrix):
    high = value.astype(BF16)
    rest = value - high.astype(F32)
    middle = rest.astype(BF16)
    low = (rest - middle.astype(F32)).astype(BF16)
    dot = functools.partial(jnp.dot, preferred_element_type=F32)
    return dot(high, matrix) + dot(middle, matrix) + dot(low, matrix)


def fine_masks():
    lane = lax.broadcasted_iota(jnp.int32, (16, 128), 1)
    row = lax.broadcasted_iota(jnp.int32, (16, 128), 0)
    return (
        lane < 112,
        lane >= 16,
        (lane % 16 < 15) & (row < 15),
        (lane % 16 >= 1) & (row >= 1),
    )


def above(pair, masks):
    low, high = (pltpu.roll(v, 112, 1) for v in pair)
    return jnp.where(masks[0], low, high), jnp.where(masks[0], high, 0.0)


def below(pair, masks):
    low, high = (pltpu.roll(v, 16, 1) for v in pair)
    return jnp.where(masks[1], low, 0.0), jnp.where(masks[1], high, low)


def mixed(v, masks):
    up = pltpu.roll(pltpu.roll(v, 127, 1), 15, 0)
    down = pltpu.roll(pltpu.roll(v, 1, 1), 1, 0)
    return v + jnp.where(masks[2], up, 0.0) + jnp.where(masks[3], down, 0.0)


def fine_conv(rows, masks):
    before, now = None, rows(0)
    for i in range(16):
        after = rows(i + 1) if i < 15 else None
        total = now
        if after is not None:
            total = tuple(a + b for a, b in zip(total, above(after, masks)))
        if before is not None:
            total = tuple(a + b for a, b in zip(total, before))
        yield i, tuple(mixed(v, masks) for v in total)
        before, now = below(now, masks), after


def coarse_conv(rows, masks):
    out = []
    for i in range(8):
        total = rows[i]
        if i < 7:
            total = total + jnp.where(masks[0], pltpu.roll(rows[i + 1], 120, 1), 0.0)
        if i > 0:
            total = total + jnp.where(masks[1], pltpu.roll(rows[i - 1], 8, 1), 0.0)
        up = pltpu.roll(pltpu.roll(total, 127, 1), 14, 0)
        down = pltpu.roll(pltpu.roll(total, 1, 1), 2, 0)
        out.append(total + jnp.where(masks[2], up, 0.0) + jnp.where(masks[3], down, 0.0))
    return out


def body(
    field,
    left_maps,
    right_maps,
    coarse_maps,
    second_scale,
    pools,
    spreads,
    lift,
    product,
    left_sums,
    right_sums,
    angles,
    sines,
    work,
    pooled,
    back,
):
    masks = fine_masks()
    halves = (slice(0, 128), slice(128, 256))
    inverse = [jnp.broadcast_to(right_maps[0:1, h], (16, 128)) for h in halves]
    scaled = [jnp.broadcast_to(right_maps[1:2, h], (16, 128)) for h in halves]
    root = [jnp.broadcast_to(right_maps[2:3, h], (16, 128)) for h in halves]

    def forward(a, carry):
        def rows(i):
            return tuple(field[i // 2, a, i % 2, :, h] for h in halves)

        held = None
        roots, inverses = left_maps[0, a], left_maps[1, a]
        for i, source in fine_conv(rows, masks):
            factor = jnp.broadcast_to(roots[:, i : i + 1], (16, 128))
            scale = jnp.broadcast_to(inverses[:, i : i + 1], (16, 128))
            kernel = []
            for n, h in enumerate(halves):
                cosine = source[n] * (scale * inverse[n])
                angle, sine = angle_and_sine(cosine)
                angles[a, i, :, h] = angle
                sines[a, i, :, h] = sine
                kernel.append((sine + angle * cosine) * (factor * scaled[n]))
            if i % 2:
                for n, h in enumerate(halves):
                    work[(i // 2) * 16 : (i // 2) * 16 + 16, h] = held[n] + kernel[n]
            held = kernel
        pooled[a] = split_dot(work[...], pools[a % 2])
        return carry

    lax.fori_loop(0, 4, forward, 0)

    lane = lax.broadcasted_iota(jnp.int32, (16, 128), 1)
    row = lax.broadcasted_iota(jnp.int32, (16, 128), 0)
    even = row % 2 == 0
    coarse_masks = (
        lane % 64 < 56,
        lane % 64 >= 8,
        (lane % 8 < 7) & (row < 14),
        (lane % 8 >= 1) & (row >= 2),
    )
    spot = lax.broadcasted_iota(jnp.int32, (8, 128), 1)
    second_left = jnp.zeros((8, 128), F32)
    second_right = jnp.zeros((16, 128), F32)
    for p in range(2):
        joined = pooled[2 * p] + pooled[2 * p + 1]
        level = []
        for i in range(8):
            v = joined[i * 16 : i * 16 + 16]
            level.append(v + jnp.where(even, pltpu.roll(v, 15, 0), pltpu.roll(v, 1, 0)))
        source = coarse_conv(level, coarse_masks)
        level = []
        for i in range(8):
            angle, sine = angle_and_sine(source[i] * coarse_maps[0, p, i])
            weighted = coarse_maps[1, p, i] * sine
            second_right = second_right + weighted
            for side in range(2):
                kept = jnp.where((lane < 64) == (side == 0), weighted, 0.0)
                total = jnp.sum(kept, axis=1, keepdims=True)
                for j in range(2):
                    place = ((2 * p + side) * 8 + i) * 2 + j
                    second_left = jnp.where(spot == place, total[j * 8 : j * 8 + 8], second_left)
            level.append(coarse_maps[2, p, i] * angle)
        for i, v in enumerate(coarse_conv(level, coarse_masks)):
            back[p, i * 16 : i * 16 + 16] = v

    def backward(a, carry):
        left_total, right_low, right_high = carry
        work[...] = split_dot(back[a // 2], spreads[a % 2])
        right = [right_low, right_high]
        roots = left_maps[0, a]
        for i in range(16):
            factor = jnp.broadcast_to(roots[:, i : i + 1], (16, 128))
            across = None
            for n, h in enumerate(halves):
                coarse = work[(i // 2) * 16 : (i // 2) * 16 + 16, h]
                product[a, i, :, h] = coarse * angles[a, i, :, h] * (1.0 / (18.0 * math.pi))
                weighted = coarse * sines[a, i, :, h]
                right[n] = right[n] + weighted * factor
                term = weighted * root[n]
                across = term if across is None else across + term
            total = jnp.sum(across, axis=1, keepdims=True)
            for j in range(2):
                place = a * 32 + i * 2 + j
                left_total = jnp.where(spot == place, total[j * 8 : j * 8 + 8], left_total)
        return left_total, right[0], right[1]

    zero = jnp.zeros((16, 128), F32)
    left_total, *right = lax.fori_loop(
        0, 4, backward, (jnp.zeros((8, 128), F32), zero, zero)
    )
    left_sums[:, 0:128] = left_total
    left_sums[:, 128:256] = second_left
    two = jnp.sum(second_right, axis=0, keepdims=True) * second_scale[...]
    lifted = jnp.dot(
        two, lift[...], precision=lax.Precision.HIGHEST, preferred_element_type=F32
    )
    for n, h in enumerate(halves):
        one = jnp.sum(right[n], axis=0, keepdims=True) * right_maps[3:4, h]
        row_sum = one + lifted[0:1, h]
        for target in range(8):
            right_sums[target, n : n + 1, :] = row_sum


def last_conv(product, left_sums, blocks):
    masks = fine_masks()
    halves = (slice(0, 128), slice(128, 256))

    def image(a, carry):
        def rows(i):
            return tuple(product[a, i, :, h] for h in halves)

        for i, source in fine_conv(rows, masks):
            first = pl.multiple_of(a * 32 + (i % 2) * 16, 16)
            for n, h in enumerate(halves):
                blocks[i // 2, pl.ds(first, 16), h] = source[n]
        return carry

    lax.fori_loop(0, 4, image, 0)
    for target in range(8):
        blocks[target, 128:136, :] = left_sums[...]


def finish_right(sums, matrix, out):
    dot = functools.partial(
        jnp.dot, precision=lax.Precision.HIGHEST, preferred_element_type=F32
    )
    mapped = dot(sums[:, 0, :], matrix[0:128, :]) + dot(sums[:, 1, :], matrix[128:256, :])
    for k in range(16):
        out[:, k, :] = mapped[:, k * 16 : k * 16 + 16]


VMEM = pl.BlockSpec(memory_space=pltpu.VMEM)


def call(kernel, out_shapes, scratch=(), held=True):
    make = pltpu.VMEM if held else jax.ShapeDtypeStruct
    shapes = tuple(make(s, F32) for s in out_shapes)

    def run(*arrays):
        return pl.pallas_call(
            kernel,
            out_shape=shapes if len(shapes) > 1 else shapes[0],
            in_specs=[VMEM] * len(arrays),
            out_specs=(VMEM,) * len(shapes) if len(shapes) > 1 else VMEM,
            scratch_shapes=[pltpu.VMEM(s, F32) for s in scratch],
            compiler_params=pltpu.CompilerParams(vmem_limit_bytes=16 << 20),
        )(*(pltpu.with_memory_space_constraint(v, pltpu.VMEM) for v in arrays))

    return run


def summed_over_pairs(part):
    part = part + lax.ppermute(part, "pair", [(p, p ^ 1) for p in range(32)])
    for stride in (2, 8):

        def moved(by):
            return lax.ppermute(
                part,
                "pair",
                [(p, p + ((p // stride + by) % 4 - p // stride % 4) * stride) for p in range(32)],
            )

        part = (part + moved(2)) + (moved(1) + moved(3))
    return part


def near(rows, columns):
    close = (jnp.abs(rows[0][:, None] - columns[0][None, :]) <= 1) & (
        jnp.abs(rows[1][:, None] - columns[1][None, :]) <= 1
    )
    return close.astype(F32) / 9.0


def on_device(gram_field, left_variance, right_variance, cotangent):
    rank = lax.axis_index("row")
    sent = jnp.transpose(gram_field, (1, 0, 2, 3, 4))
    field = lax.all_to_all(sent, "row", split_axis=0, concat_axis=0, tiled=True)

    first_left = conv_map(left_variance)
    own_right = lax.dynamic_slice_in_dim(right_variance, rank, 1, axis=0)
    first_right = conv_map(own_right)
    second_left = conv_map(pool_map(first_left / 2.0))
    second_right = conv_map(pool_map(first_right / 2.0)).reshape(64)
    left_root = jnp.swapaxes(jnp.sqrt(first_left), -1, -2)
    left_maps = jnp.stack([left_root, 1.0 / (9.0 * left_root)])
    right_root = jnp.sqrt(first_right).reshape(1, 256)
    right_maps = jnp.concatenate(
        [
            1.0 / right_root,
            right_root / (32.0 * math.pi),
            right_root,
            1.0 / (4.0 * math.pi * right_root),
        ]
        * 2,
        axis=0,
    )

    def packed(v):
        v = jnp.repeat(v.reshape(2, 2, 8, 8, 64), 2, axis=3)
        return jnp.concatenate([v[:, 0], v[:, 1]], axis=-1)

    second = jnp.sqrt(second_left)[..., None] * jnp.sqrt(second_right)
    cotangent = cotangent[:, 0]
    coarse_maps = jnp.stack(
        [
            packed(1.0 / (9.0 * second)),
            packed(cotangent * second / (4.0 * math.pi)),
            packed(cotangent / (2.0 * math.pi * 9.0 * 16.0)),
        ]
    )
    second_scale = jnp.broadcast_to(jnp.tile(0.5 / second_right, 2)[None], (1, 128))

    fine = jnp.arange(256)
    small = jnp.arange(64)
    coarse_of = (fine // 32) * 8 + (fine % 16) // 2
    pool = (coarse_of[:, None] == small[None, :]).astype(BF16)
    nothing = jnp.zeros_like(pool)
    pools = jnp.stack(
        [jnp.concatenate([pool, nothing], 1), jnp.concatenate([nothing, pool], 1)]
    )
    spreads = jnp.transpose(pools, (0, 2, 1))
    lift = near((small // 8, small % 8), (coarse_of // 8, coarse_of % 8)) / 8.0
    lift = jnp.concatenate([lift, lift], axis=0)
    around = near((fine // 16, fine % 16), (fine // 16, fine % 16))

    product, left_sums, right_sums = call(
        body,
        ((4, 16, 16, 256), (8, 256), (8, 2, 128)),
        (
            (4, 16, 16, 256),
            (4, 16, 16, 256),
            (128, 256),
            (4, 128, 128),
            (2, 128, 128),
        ),
    )(field, left_maps, right_maps, coarse_maps, second_scale, pools, spreads, lift)
    right_all = lax.all_to_all(right_sums, "row", split_axis=0, concat_axis=0, tiled=True)
    blocks = call(last_conv, ((8, 136, 256),))(product, left_sums)
    right_all, blocks = lax.optimization_barrier((right_all, blocks))
    blocks = lax.all_to_all(blocks, "row", split_axis=0, concat_axis=0, tiled=True)
    right_all = summed_over_pairs(right_all)
    gram_gradient = jnp.transpose(blocks[:, :128].reshape(8, 4, 2, 16, 256), (1, 0, 2, 3, 4))

    left_all = jnp.sum(blocks[:, 128:], axis=0)
    left_one = left_all[:, :128].reshape(8, 4, 16, 2).transpose(1, 2, 3, 0).reshape(4, 16, 16)
    left_two = left_all[:, 128:192].reshape(4, 2, 4, 8, 2)[:, 0]
    left_two = left_two.transpose(1, 2, 3, 0).reshape(4, 8, 8)
    left_one = left_one / (4.0 * math.pi * jnp.sqrt(first_left))
    left_one = left_one + spread_map(conv_map(left_two / second_left)) / 2.0
    left_gradient = conv_map(left_one)
    right_all, gram_gradient, left_gradient = lax.optimization_barrier(
        (right_all, gram_gradient, left_gradient)
    )
    right_gradient = call(finish_right, ((8, 16, 16),), held=False)(right_all, around)
    return gram_gradient, left_gradient, right_gradient


def solution(mesh):
    in_specs = (
        P("pair", None, "row", None, None),
        P("pair", None, None),
        P(),
        P("pair", "row", None, None, None),
    )
    out_specs = (P("pair", None, "row", None, None), P("pair", None, None), P())
    return jax.shard_map(
        on_device, mesh=mesh, in_specs=in_specs, out_specs=out_specs, check_vma=False
    )
```
